32 devices in a mesh: rows: 8 (over y, x, core), tp: 4 (over z).
Axes of the slice: x: 2, y: 2, z: 4, core: 2. Of those that a mesh axis runs over, the one named last changes fastest.
Arguments:
- features: bfloat16 [16384, 768], P('rows'), may hold values from -6 to 6
- type_ids: int32 [16384], P('rows'), may hold values 0 or 1
- segment_ids: int32 [32, 512], P('rows'), may hold values from 0 to 3, never falling along the last dimension, each value on 1 to 256 neighbouring positions
- type_table: bfloat16 [2, 768], replicated, may hold values from -3 to 3
- w_qkv: bfloat16 [3, 768, 768], P(None, None, 'tp'), may hold values from -0.3125 to 0.3125
- b_qv: bfloat16 [2, 768], P(None, 'tp'), may hold values from -3 to 3
- w_out: bfloat16 [768, 768], P('tp'), may hold values from -0.875 to 0.875
- b_out: bfloat16 [768], replicated, may hold values from -3 to 3
- gain_attn: bfloat16 [768], replicated, may hold values from 0.25 to 1.75
- shift_attn: bfloat16 [768], replicated, may hold values from -3 to 3
- w_up: bfloat16 [768, 3072], P(None, 'tp'), may hold values from -0.21875 to 0.21875
- b_up: bfloat16 [3072], P('tp'), may hold values from -3 to 3
- w_down: bfloat16 [3072, 768], P('tp'), may hold values from -0.109375 to 0.109375
- b_down: bfloat16 [768], replicated, may hold values from -3 to 3
- gain_ffn: bfloat16 [768], replicated, may hold values from 0.25 to 1.75
- shift_ffn: bfloat16 [768], replicated, may hold values from -3 to 3
- cotangent: bfloat16 [16384, 768], P('rows'), may hold values from -6 to 6
Outputs:
- output: bfloat16 [16384, 768], P('rows')
- grad_features: bfloat16 [16384, 768], P('rows')
- grad_table: float32 [2, 768], replicated
- grad_qkv: float32 [3, 768, 768], P(None, None, 'tp')
- grad_bias_qv: float32 [2, 768], P(None, 'tp')
- grad_w_out: float32 [768, 768], P('tp')
- grad_b_out: float32 [768], replicated
- grad_gain_attn: float32 [768], replicated
- grad_shift_attn: float32 [768], replicated
- grad_w_up: float32 [768, 3072], P(None, 'tp')
- grad_b_up: float32 [3072], P('tp')
- grad_w_down: float32 [3072, 768], P('tp')
- grad_b_down: float32 [768], replicated
- grad_gain_ffn: float32 [768], replicated
- grad_shift_ffn: float32 [768], replicated
The draws below stay inside these ranges and needn't reach their ends.
Inputs may be any that keep to these rules, and one draw needn't show every extreme that they name: `segment_ids`: along each packed row the ids never fall; each of the 4 ids covers 1 to 256 tokens, and one covers exactly 256.
All inputs are finite; a program needn't handle non-finite values. No bound on the sum of `type_ids` on one device may be relied on, other than what follows from the above.
Results may differ from the reference program's by a relative error of at most 0.015.
The reference program's roundings to bfloat16 on the way count: a program that leaves them out, or rounds other values in their place, can miss the bound.
Values sent between devices are 32-bit elements; how exact they have to be, the bound alone decides.
No kernel may reach another device: no remote copies, remote signals or barrier semaphores. Data moves between devices by JAX's collectives and lax.ppermute only.
A program may use at most 128 MiB of HBM per device.

```python
import math
import jax
import jax.numpy as jnp
import numpy as np
from jax import lax

D = 768
HEADS = 12
HEAD_DIM = 64
FF = 3072
LENGTH = 512
SEGS = 4
ROWS = 32
TOKENS = 16384


def set_ends(array, own_key, smallest, high):
    longest = array.shape.index(max(array.shape))
    spots = []
    for shift in (0, 1):
        where = [jax.random.randint(jax.random.fold_in(own_key, axis), (), 0, length) for axis, length in enumerate(array.shape)]
        where[longest] = (where[longest] + shift) % array.shape[longest]
        spots.append(tuple(where))
    return array.at[spots[0]].set(smallest).at[spots[1]].set(high)


def shard_levels(own_key, extent, cuts, least, top_value):
    factor_of, own = 1.0, jax.random.fold_in(own_key, 6)
    for axis_at, parts in cuts:
        steps = jnp.exp(jax.random.uniform(jax.random.fold_in(own, axis_at), (parts,), jnp.float32, least / len(cuts), top_value / len(cuts)))
        factor_of = factor_of * jnp.repeat(steps, extent[axis_at] // parts).reshape([-1 if axis == axis_at else 1 for axis in range(len(extent))])
    return factor_of


def length_profile(amount, total, bound, slope):
    loads = [(1 << 20) // math.isqrt(grade ** slope) + 1 for grade in range(2, amount + 1)]
    surplus, counts = total - bound - (amount - 1), [1] * (amount - 1)
    while surplus > 0:
        free = [i for i in range(amount - 1) if counts[i] < bound]
        pool, budget = sum([loads[i] for i in free]), surplus
        for i in free:
            addition = min(bound - counts[i], max(1, budget * loads[i] // pool), surplus)
            counts[i] = counts[i] + addition
            surplus = surplus - addition
    return np.array([bound] + counts)


def uneven(key, count, total, bound, lean):
    if count == 2:
        one = jax.random.randint(key, (), max(1, total - bound), min(bound, total - 1) + 1)
        return jnp.stack([one, total - one])
    lengths = jnp.asarray(length_profile(count, total, bound, lean), jnp.int32)
    twos = (count - 1) // 2
    donor, taker = lengths[1:1 + 2 * twos:2], lengths[2:2 + 2 * twos:2]
    margin = jnp.minimum(donor - 1, bound - taker)
    moved = jax.random.randint(jax.random.fold_in(key, 1), (twos,), 0, 1 << 20) % (margin + 1)
    lengths = lengths.at[1:1 + 2 * twos:2].set(donor - moved).at[2:2 + 2 * twos:2].set(taker + moved)
    return lengths[jax.random.permutation(jax.random.fold_in(key, 2), count)]


def scatter_about(rng, extent, deviation, limit, cuts=(), dtype=jnp.bfloat16):
    entries = jax.random.normal(rng, extent, jnp.float32) * deviation
    if len(cuts) > 0:
        entries = shard_levels(rng, extent, cuts, -0.22, 0.18) * entries
    return jnp.clip(entries, min=-limit, max=limit).astype(dtype)


def setup_inputs(seed: int = 0) -> dict:
    seeds = jax.random.split(jax.random.key(seed), 18)
    return {
        "features": scatter_about(seeds[0], (TOKENS, D), 1.0, 6.0, ((0, 8),)),
        "type_ids": set_ends((jax.random.randint(seeds[1], (TOKENS,), 0, 3) < 1).astype(jnp.int32), jax.random.fold_in(seeds[1], 1), 0, 1),
        "segment_ids": jax.vmap(lambda own: jnp.searchsorted(jnp.cumsum(uneven(own, SEGS, LENGTH, LENGTH // 2, 0)), jnp.arange(LENGTH), side="right"))(jax.random.split(seeds[2], ROWS)).reshape((ROWS, LENGTH)).astype(jnp.int32),
        "type_table": scatter_about(seeds[3], (2, D), 0.5, 3.0),
        "w_qkv": scatter_about(seeds[4], (3, D, D), (D // 2) ** -0.5, 0.3125, ((2, 4),)),
        "b_qv": scatter_about(seeds[5], (2, D), 0.5, 3.0, ((1, 4),)),
        "w_out": scatter_about(seeds[6], (D, D), (D // 16) ** -0.5, 0.875, ((0, 4),)),
        "b_out": scatter_about(seeds[7], (D,), 0.5, 3.0),
        "gain_attn": jnp.clip(1.0 + 0.15 * jax.random.normal(seeds[8], (D,), jnp.float32), 0.25, 1.75).astype(jnp.bfloat16),
        "shift_attn": scatter_about(seeds[9], (D,), 0.5, 3.0),
        "w_up": scatter_about(seeds[10], (D, FF), D ** -0.5, 0.21875, ((1, 4),)),
        "b_up": scatter_about(seeds[11], (FF,), 0.5, 3.0, ((0, 4),)),
        "w_down": scatter_about(seeds[12], (FF, D), FF ** -0.5, 0.109375, ((0, 4),)),
        "b_down": scatter_about(seeds[13], (D,), 0.5, 3.0),
        "gain_ffn": jnp.clip(1.0 + 0.15 * jax.random.normal(seeds[14], (D,), jnp.float32), 0.25, 1.75).astype(jnp.bfloat16),
        "shift_ffn": scatter_about(seeds[15], (D,), 0.5, 3.0),
        "cotangent": scatter_about(seeds[16], (TOKENS, D), 1.0, 6.0, ((0, 8),)),
    }


highest = lax.Precision.HIGHEST

@jax.custom_vjp
def low(v):
    return lax.optimization_barrier(v.astype(jnp.bfloat16)).astype(jnp.float32)

@jax.custom_vjp
def low_back(v):
    return v

def low_keep(v):
    return (low(v), None)

def low_pass(kept, grad):
    return (grad,)

def back_keep(v):
    return (v, None)

def back_low(kept, grad):
    return (low(grad),)
low.defvjp(low_keep, low_pass)
low_back.defvjp(back_keep, back_low)

def normalize(hidden):
    center = hidden - lax.optimization_barrier(jnp.mean(hidden, axis=-1, keepdims=True))
    variance = lax.optimization_barrier(jnp.mean(center * center, axis=-1, keepdims=True))
    return center * lax.rsqrt(variance + 1e-05)

def attend_row(packed):
    queries, keys_row, values, segment = packed
    scores = jnp.einsum('qhd,khd->hqk', queries, keys_row, precision=highest) * HEAD_DIM ** (-0.5)
    scores = low_back(scores)
    same_doc = segment[:, None] == segment[None, :]
    masked = jnp.where(same_doc[None], scores, -1000000000.0)
    shifted = masked - lax.optimization_barrier(jnp.max(masked, axis=-1, keepdims=True))
    weights = jnp.exp(shifted)
    weights = weights / lax.optimization_barrier(jnp.sum(weights, axis=-1, keepdims=True))
    return jnp.einsum('hqk,khd->qhd', low(weights), values, precision=highest)

def layer(features, params, type_frac, segments):
    type_table, w_qkv, b_qv, w_out, b_out, gain_attn, shift_attn, w_up, b_up, w_down, b_down, gain_ffn, shift_ffn = params
    embedded = features + (type_table[0] + type_frac * (type_table[1] - type_table[0]))
    normal_in = low(embedded)
    queries = low(low_back(jnp.dot(normal_in, w_qkv[0], precision=highest) + b_qv[0]))
    keys_all = low(low_back(jnp.dot(normal_in, w_qkv[1], precision=highest)))
    values = low(low_back(jnp.dot(normal_in, w_qkv[2], precision=highest) + b_qv[1]))
    group = segments.shape[0]
    shape_four = (group, LENGTH, HEADS, HEAD_DIM)
    attended = lax.map(jax.checkpoint(attend_row), (queries.reshape(shape_four), keys_all.reshape(shape_four), values.reshape(shape_four), segments))
    attended = low(low_back(attended.reshape(group * LENGTH, D)))
    attn_out = low_back(jnp.dot(attended, w_out, precision=highest)) + b_out
    normed_one = normalize(embedded + attn_out) * gain_attn + shift_attn
    pre_act = low_back(jnp.dot(low(normed_one), w_up, precision=highest) + b_up)
    activated = low(jax.nn.gelu(pre_act, approximate=False))
    ffn_out = low_back(jnp.dot(activated, w_down, precision=highest)) + b_down
    return normalize(normed_one + ffn_out) * gain_ffn + shift_ffn

def reference(features, type_ids, segment_ids, type_table, w_qkv, b_qv, w_out, b_out, gain_attn, shift_attn, w_up, b_up, w_down, b_down, gain_ffn, shift_ffn, cotangent):
    params = tuple((item.astype(jnp.float32) for item in (type_table, w_qkv, b_qv, w_out, b_out, gain_attn, shift_attn, w_up, b_up, w_down, b_down, gain_ffn, shift_ffn)))
    group = math.gcd(ROWS, 8)
    groups = ROWS // group
    width = group * LENGTH
    feats = features.astype(jnp.float32).reshape(groups, width, D)
    types = type_ids.astype(jnp.float32).reshape(groups, width, 1)
    segs = segment_ids.reshape(groups, group, LENGTH)
    cotans = cotangent.astype(jnp.float32).reshape(groups, width, D)

    def step_group(totals, item):
        feat_group, type_group, seg_group, cotan_group = item
        result, pull = jax.vjp(lambda inner, weights: layer(inner, weights, type_group, seg_group), feat_group, params)
        grad_inner, grad_params = pull(cotan_group)
        totals = jax.tree.map(lambda left, right: left + right, totals, grad_params)
        return (totals, (result.astype(jnp.bfloat16), grad_inner.astype(jnp.bfloat16)))
    start = jax.tree.map(lambda item: jnp.zeros_like(item), params)
    totals, (results, grads_in) = lax.scan(step_group, start, (feats, types, segs, cotans))
    return (results.reshape(TOKENS, D), grads_in.reshape(TOKENS, D), totals[0], totals[1], totals[2], totals[3], totals[4], totals[5], totals[6], totals[7], totals[8], totals[9], totals[10], totals[11], totals[12])
```

```python
import jax
import jax.numpy as jnp
from jax import lax
from jax.experimental import pallas as pl
from jax.sharding import PartitionSpec as P

HEAD_DIM = 64
BITS = 3
PIECES = 1 << BITS
NEG = -1000000000.0


def normalize(hidden):
    center = hidden - jnp.mean(hidden, axis=-1, keepdims=True)
    variance = jnp.mean(center * center, axis=-1, keepdims=True)
    inverse = lax.rsqrt(variance + 1e-05)
    return (center * inverse, inverse)


def norm_back(grad_norm, normed, inverse):
    mean_grad = jnp.mean(grad_norm, axis=-1, keepdims=True)
    mean_proj = jnp.mean(grad_norm * normed, axis=-1, keepdims=True)
    return inverse * (grad_norm - mean_grad - normed * mean_proj)


def f32(x):
    return x.astype(jnp.float32)


def bf16(x):
    return x.astype(jnp.bfloat16)


def round_kernel(x_ref, o_ref):
    o_ref[...] = x_ref[...].astype(jnp.bfloat16)


def rounded(x):
    n, d = x.shape
    block = n // 4
    return pl.pallas_call(
        round_kernel,
        grid=(4,),
        in_specs=[pl.BlockSpec((block, d), lambda i: (i, 0))],
        out_specs=pl.BlockSpec((block, d), lambda i: (i, 0)),
        out_shape=jax.ShapeDtypeStruct((n, d), jnp.bfloat16),
    )(x)


def join_ffn_kernel(own_ref, mine_ref, other_ref, o_ref):
    o_ref[0, :, 0, :, 0] = own_ref[0, :, :, 0].astype(jnp.bfloat16)
    o_ref[0, 0, 0, :, 1:] = mine_ref[0, :, :, 0].astype(jnp.bfloat16)
    o_ref[0, 1, 0, :, 1:] = other_ref[0, :, :, 0].astype(jnp.bfloat16)


def join_ffn(own, mine, other):
    _, quads, others, _, n, d = mine.shape
    spec = pl.BlockSpec((1, quads, others, 1, n, d), lambda i, s: (s, 0, 0, i, 0, 0))
    return pl.pallas_call(
        join_ffn_kernel,
        grid=(2, 2),
        in_specs=[
            pl.BlockSpec((1, 2, quads, 1, n, d), lambda i, s: (s, 0, 0, i, 0, 0)),
            spec,
            spec,
        ],
        out_specs=pl.BlockSpec(
            (1, 2, 1, quads, others + 1, n, d), lambda i, s: (i, 0, s, 0, 0, 0, 0)
        ),
        out_shape=jax.ShapeDtypeStruct((2, 2, 2, quads, others + 1, n, d), jnp.bfloat16),
    )(own, mine, other)


def join_att_kernel(own_ref, mine_ref, other_ref, o_ref):
    _, pieces, _, heads, _, _ = own_ref.shape
    quads, others = mine_ref.shape[1:3]
    for h in range(heads):
        parts = [own_ref[0, j, 0, h] for j in range(pieces)]
        o_ref[0, 0, 0, h] = jnp.concatenate(parts).astype(jnp.bfloat16)
        for t in range(others):
            parts = [ref[0, j, t, 0, h] for ref in (mine_ref, other_ref) for j in range(quads)]
            o_ref[0, 0, t + 1, h] = jnp.concatenate(parts).astype(jnp.bfloat16)


def join_att(own, mine, other):
    _, quads, others, _, heads, e, d = mine.shape
    pieces = own.shape[1]
    spec = pl.BlockSpec((1, quads, others, 1, heads, e, d), lambda s, i: (s, 0, 0, i, 0, 0, 0))
    return pl.pallas_call(
        join_att_kernel,
        grid=(2, 2),
        in_specs=[
            pl.BlockSpec((1, pieces, 1, heads, e, d), lambda s, i: (s, 0, i, 0, 0, 0)),
            spec,
            spec,
        ],
        out_specs=pl.BlockSpec(
            (1, 1, others + 1, heads, pieces * e, d), lambda s, i: (s, i, 0, 0, 0, 0)
        ),
        out_shape=jax.ShapeDtypeStruct((2, 2, others + 1, heads, pieces * e, d), jnp.bfloat16),
    )(own, mine, other)


def dot_t(a, b):
    return lax.dot_general(a, b, (((1,), (1,)), ((), ())), preferred_element_type=jnp.float32)


def dot_n(a, b):
    return lax.dot_general(a, b, (((1,), (0,)), ((), ())), preferred_element_type=jnp.float32)


def dot_a(a, b):
    return lax.dot_general(a, b, (((0,), (0,)), ((), ())), preferred_element_type=jnp.float32)


def make(mesh):
    rows = mesh.shape["rows"]
    T = mesh.shape["tp"]
    row_bits = rows.bit_length() - 1

    def swap(x, bit):
        return lax.ppermute(x, "rows", [(i, i ^ (1 << bit)) for i in range(rows)])

    def z_right(x, low):
        return lax.ppermute(x, "tp", [(i - 1, i) for i in range(low, T)])

    def z_left(x, high):
        return lax.ppermute(x, "tp", [(i + 1, i) for i in range(high)])

    def gather(piece):
        right, left, rs, ls = piece, piece, [], []
        for k in range(1, T):
            right = z_right(right, k)
            left = z_left(left, T - k)
            rs.append(right)
            ls.append(left)
        out = []
        for s, order in ((0, (1, 2)), (1, (2, 1))):
            buf = jnp.stack([rs[k - 1][s] + ls[T - k - 1][s] for k in range(1, T)])
            for bit in order:
                buf = jnp.stack([buf, swap(buf, bit)])
            out.append(buf)
        both = jnp.stack(out)
        return both, swap(both, 0)

    def reduce_scatter(keep, send):
        both = keep + swap(send, 0)
        outs = []
        for s, order in ((0, (2, 1)), (1, (1, 2))):
            acc = both[s]
            for bit in order:
                acc = acc[0] + swap(acc[1], bit)
            outs.append(acc)
        acc = jnp.stack(outs, axis=1)
        right = acc[1]
        left = acc[T - 1]
        for k in range(T - 1, 0, -1):
            right = lax.ppermute(right, "tp", [(i, i + 1) for i in range(T - k)])
            left = lax.ppermute(left, "tp", [(i + k, i + k - 1) for i in range(T - k)])
            nxt = (T - (k - 1)) % T
            if k > 1:
                right = right + acc[nxt]
                left = left + acc[k - 1]
        total = acc[0] + right + left
        for bit in range(BITS, row_bits):
            total = total + swap(total, bit)
        return total

    def spread(total):
        out = []
        for s, order in ((0, (1, 2)), (1, (2, 1))):
            buf = total[s]
            for bit in order:
                buf = jnp.stack([buf, swap(buf, bit)])
            out.append(buf)
        both = jnp.stack(out)
        return jnp.stack([both, swap(both, 0)])

    def per_device(
        features, type_ids, segment_ids, type_table, w_qkv, b_qv, w_out, b_out, gain_attn,
        shift_attn, w_up, b_up, w_down, b_down, gain_ffn, shift_ffn, cotangent,
    ):
        z = lax.axis_index("tp")
        r = lax.axis_index("rows")
        bits = [(r >> b) & 1 for b in range(BITS)]
        mask_a = bits[0] * 4 + bits[2] * 2 + bits[1]
        mask_b = bits[0] * 4 + bits[1] * 2 + bits[2]
        masks = (mask_a, mask_b)
        D = features.shape[1]
        width = w_qkv.shape[2]
        heads = width // HEAD_DIM
        shard_ff = w_up.shape[1]
        tokens = features.shape[0] // T
        length = segment_ids.shape[1]
        nrows = segment_ids.shape[0] // T
        E = HEAD_DIM // PIECES
        FP = shard_ff // (2 * PIECES)

        def own_slice(x, n):
            return lax.dynamic_slice_in_dim(x, z * n, n, 0)

        def reorder(x, mask, axis):
            return jnp.concatenate(
                [lax.dynamic_slice_in_dim(x, i ^ mask, 1, axis) for i in range(PIECES)], axis
            )

        def z_rel(x):
            return jnp.stack(
                [
                    sum(jnp.where((z - k) % T == a, x[a], 0.0) for a in range(T))
                    for k in range(T)
                ]
            )

        def flip(x, axis, mask):
            for b in range(BITS):
                on = ((mask >> b) & 1) == 1
                x = x.reshape(x.shape[:axis] + (PIECES >> (b + 1), 2, 1 << b) + x.shape[axis + 1 :])
                parts = jnp.split(x, 2, axis + 1)
                x = jnp.where(on, jnp.concatenate(parts[::-1], axis + 1), x)
                x = x.reshape(x.shape[:axis] + (PIECES,) + x.shape[axis + 3 :])
            return x

        qkv_t = f32(jnp.swapaxes(w_qkv, 1, 2))
        att4 = jnp.concatenate([qkv_t, f32(w_out)[None]]).reshape(2, 2, heads, PIECES, E, D)
        att_own = jnp.stack(
            [reorder(att4[s].transpose(2, 0, 1, 3, 4), masks[s], 0) for s in (0, 1)]
        )
        ffn2 = jnp.stack([f32(w_up.T), f32(w_down)]).reshape(2, 2, PIECES, FP, D)
        ffn_own = jnp.stack(
            [reorder(ffn2[:, s].transpose(1, 0, 2, 3), masks[s], 0) for s in (0, 1)]
        )
        na, nf = 2 * heads * E, 2 * FP
        att_own = lax.optimization_barrier(att_own)
        ffn_own = lax.optimization_barrier(ffn_own)
        quads = PIECES // 2
        shape = (2, quads, T - 1, 2, heads, E, D)
        att_all = gather(att_own[:, 0].reshape(2, na, D))
        ffn_all = gather(ffn_own[:, 0].reshape(2, nf, D))
        att_w = join_att(att_own, *(x.reshape(shape) for x in att_all))
        att_w = att_w.reshape(4 * T * width, D)
        wqkv_t = att_w[: 3 * T * width]
        wo = att_w[3 * T * width :]
        shape = (2, quads, T - 1, 2, FP, D)
        ffn_w = join_ffn(
            ffn_own.reshape(2, 2, quads, 2, FP, D), *(x.reshape(shape) for x in ffn_all)
        )
        ffn_w = ffn_w.reshape(2, T * shard_ff, D)
        up_t, down = ffn_w[0], ffn_w[1]

        small = jnp.concatenate([f32(b_qv).reshape(-1), f32(b_up)])
        small = lax.all_gather(small, "tp", axis=0)
        bqv_abs = small[:, : 2 * width].reshape(T, 2, heads, PIECES, E)
        bup_abs = small[:, 2 * width :].reshape(T, 2, PIECES, FP)
        bqv_rel = z_rel(bqv_abs)
        bq = flip(bqv_rel[:, 0], 2, mask_a).reshape(-1)
        bv = flip(bqv_rel[:, 1], 2, mask_b).reshape(-1)
        bup_rel = z_rel(bup_abs)
        bup = jnp.stack(
            [flip(bup_rel[:, s], 1, masks[s]).reshape(T, 2, 4, FP) for s in (0, 1)], 0
        )
        bup = bup.transpose(2, 0, 3, 1, 4).reshape(-1)

        type_frac = f32(own_slice(type_ids, tokens))[:, None]
        segment = own_slice(segment_ids, nrows)
        table = f32(type_table)
        embedded = f32(own_slice(features, tokens)) + (table[0] + type_frac * (table[1] - table[0]))
        normal_in = bf16(embedded)
        C = T * width
        H = T * heads
        proj = dot_t(normal_in, wqkv_t)
        shape_four = (nrows, length, H, HEAD_DIM)
        queries = bf16(proj[:, :C] + bq).reshape(shape_four)
        keys = bf16(proj[:, C : 2 * C]).reshape(shape_four)
        values = bf16(proj[:, 2 * C :] + bv).reshape(shape_four)
        scale = HEAD_DIM ** (-0.5)
        same = (segment[:, :, None] == segment[:, None, :])[:, None]
        scores = jnp.einsum("rqhd,rkhd->rhqk", queries, keys, preferred_element_type=jnp.float32)
        scores = jnp.where(same, scores * scale, NEG)
        highest = jnp.max(scores, axis=-1, keepdims=True)
        weights = jnp.exp(scores - highest)
        total = jnp.sum(weights, axis=-1, keepdims=True)
        weights = bf16(weights / total)
        attended = bf16(
            jnp.einsum("rhqk,rkhd->rqhd", weights, values, preferred_element_type=jnp.float32)
        ).reshape(tokens, C)
        attn_out = dot_n(attended, wo) + f32(b_out)
        normed_a, inverse_a = normalize(embedded + attn_out)
        gain_one = f32(gain_attn)
        normed_one = normed_a * gain_one + f32(shift_attn)
        ffn_in = bf16(normed_one)
        pre_act = dot_t(ffn_in, up_t) + bup
        cdf = 0.5 * (1.0 + lax.erf(pre_act * (0.5**0.5)))
        activated = bf16(pre_act * cdf)
        ffn_out = dot_n(activated, down) + f32(b_down)
        normed_b, inverse_b = normalize(normed_one + ffn_out)
        gain_two = f32(gain_ffn)
        out_own = normed_b * gain_two + f32(shift_ffn)
        output = rounded(lax.all_gather(out_own, "tp", axis=0, tiled=True))

        grad_out = f32(own_slice(cotangent, tokens))
        grad_shift_ffn = jnp.sum(grad_out, axis=0)
        grad_gain_ffn = jnp.sum(grad_out * normed_b, axis=0)
        grad_h2 = norm_back(grad_out * gain_two, normed_b, inverse_b)
        grad_b_down = jnp.sum(grad_h2, axis=0)
        grad_h2_low = bf16(grad_h2)
        half = T * shard_ff // 2
        six = (2, 2, 2, T, FP, D)
        gd_send = dot_a(activated[:, half:], grad_h2_low).reshape(six)
        gd_keep = dot_a(activated[:, :half], grad_h2_low).reshape(six)
        gd = reduce_scatter(gd_keep, gd_send)
        grad_act = dot_t(grad_h2_low, down)
        pdf = jnp.exp(-0.5 * pre_act * pre_act) * (0.5 / jnp.pi) ** 0.5
        grad_pre = bf16(grad_act * (cdf + pre_act * pdf))
        grad_b_up = jnp.sum(f32(grad_pre), axis=0)
        gu_send = dot_a(grad_pre[:, half:], ffn_in).reshape(six)
        gu_keep = dot_a(grad_pre[:, :half], ffn_in).reshape(six)
        gu = reduce_scatter(gu_keep, gu_send)
        grad_normed = grad_h2 + dot_n(grad_pre, up_t)
        grad_shift_attn = jnp.sum(grad_normed, axis=0)
        grad_gain_attn = jnp.sum(grad_normed * normed_a, axis=0)
        grad_h1 = norm_back(grad_normed * gain_one, normed_a, inverse_a)
        grad_b_out = jnp.sum(grad_h1, axis=0)
        grad_h1_low = bf16(grad_h1)
        grad_wo = dot_a(attended, grad_h1_low)
        grad_att = bf16(dot_t(grad_h1_low, wo)).reshape(shape_four)
        logsum = highest + jnp.log(total)
        probs = jnp.exp(scores - logsum)
        grad_weights = jnp.einsum(
            "rqhd,rkhd->rhqk", grad_att, values, preferred_element_type=jnp.float32
        )
        inner = jnp.sum(probs * grad_weights, axis=-1, keepdims=True)
        grad_scores = bf16(probs * (grad_weights - inner))
        grad_q = bf16(
            jnp.einsum("rhqk,rkhd->rqhd", grad_scores, keys, preferred_element_type=jnp.float32)
            * scale
        ).reshape(tokens, C)
        grad_k = bf16(
            jnp.einsum("rhqk,rqhd->rkhd", grad_scores, queries, preferred_element_type=jnp.float32)
            * scale
        ).reshape(tokens, C)
        grad_v = bf16(
            jnp.einsum(
                "rhqk,rqhd->rkhd", bf16(probs), grad_att, preferred_element_type=jnp.float32
            )
        ).reshape(tokens, C)
        grad_proj = jnp.concatenate([grad_q, grad_k, grad_v], axis=1)
        grad_embedded = grad_h1 + dot_n(grad_proj, wqkv_t)
        grad_features = rounded(lax.all_gather(grad_embedded, "tp", axis=0, tiled=True))
        gq = dot_a(grad_proj, normal_in)
        ga = jnp.concatenate([gq, grad_wo]).reshape(2, 2, T, heads, 2, 2, 2, E, D)
        ga = ga.transpose(4, 0, 5, 6, 2, 1, 3, 7, 8).reshape(2, 2, 2, 2, T, na, D)
        ga = reduce_scatter(ga[0], ga[1])

        mine = spread(jnp.concatenate([ga, gu, gd], axis=1))
        mine = mine.transpose(1, 0, 2, 3, 4, 5).reshape(2, PIECES, na + nf, D)
        mine = jnp.stack([reorder(mine[s], masks[s], 0) for s in (0, 1)])
        g_att = mine[:, :, :na].reshape(2, PIECES, 2, heads, E, D)
        g_att = g_att.transpose(0, 2, 3, 1, 4, 5).reshape(4, width, D)
        grad_qkv = jnp.swapaxes(g_att[:3], 1, 2)
        grad_w_out = g_att[3]
        grad_w_up = mine[:, :, na : na + FP].reshape(shard_ff, D).T
        grad_w_down = mine[:, :, na + FP :].reshape(shard_ff, D)

        gbup = grad_b_up.reshape(2, 2, 4, T, FP).transpose(1, 3, 0, 2, 4).reshape(2, T, PIECES, FP)
        gbup = jnp.stack([flip(gbup[s], 1, masks[s]) for s in (0, 1)], 1)
        gbup = z_rel(gbup).reshape(-1)
        gbq = jnp.sum(f32(grad_q), axis=0).reshape(T, heads, PIECES, E)
        gbv = jnp.sum(f32(grad_v), axis=0).reshape(T, heads, PIECES, E)
        gbq = z_rel(flip(gbq, 2, mask_a)).reshape(-1)
        gbv = z_rel(flip(gbv, 2, mask_b)).reshape(-1)
        upper = jnp.sum(type_frac * grad_embedded, axis=0)
        lower = jnp.sum(grad_embedded, axis=0) - upper
        vec = jnp.concatenate(
            [
                lower, upper, grad_b_out, grad_gain_attn, grad_shift_attn, grad_b_down,
                grad_gain_ffn, grad_shift_ffn, gbq, gbv, gbup,
            ]
        )
        vec = lax.psum(vec, ("rows", "tp"))
        lines = vec[: 8 * D].reshape(8, D)
        gb = vec[8 * D : 8 * D + 2 * C].reshape(2, C)
        grad_bias_qv = lax.dynamic_slice_in_dim(gb, z * width, width, 1)
        grad_b_up = lax.dynamic_slice_in_dim(vec[8 * D + 2 * C :], z * shard_ff, shard_ff, 0)
        return (
            output, grad_features, lines[:2], grad_qkv, grad_bias_qv, grad_w_out, lines[2],
            lines[3], lines[4], grad_w_up, grad_b_up, grad_w_down, lines[5], lines[6], lines[7],
        )

    return per_device


def solution(mesh):
    in_specs = (
        P("rows", None), P("rows"), P("rows", None), P(), P(None, None, "tp"), P(None, "tp"),
        P("tp", None), P(), P(), P(), P(None, "tp"), P("tp"), P("tp", None), P(), P(), P(),
        P("rows", None),
    )
    out_specs = (
        P("rows", None), P("rows", None), P(), P(None, None, "tp"), P(None, "tp"), P("tp", None),
        P(), P(), P(), P(None, "tp"), P("tp"), P("tp", None), P(), P(), P(),
    )
    return jax.shard_map(
        make(mesh), mesh=mesh, in_specs=in_specs, out_specs=out_specs, check_vma=False
    )
```

```python
from functools import partial

import jax
import jax.numpy as jnp
from jax import lax
from jax.experimental import pallas as pl
from jax.experimental.pallas import tpu as pltpu
from jax.sharding import PartitionSpec as P


HEAD_DIM = 64
BITS = 3
PIECES = 1 << BITS
NEG = -1000000000.0


def normalize(hidden):
    center = hidden - jnp.mean(hidden, axis=-1, keepdims=True)
    variance = jnp.mean(center * center, axis=-1, keepdims=True)
    inverse = lax.rsqrt(variance + 1e-05)
    return (center * inverse, inverse)


def norm_back(grad_norm, normed, inverse):
    mean_grad = jnp.mean(grad_norm, axis=-1, keepdims=True)
    mean_proj = jnp.mean(grad_norm * normed, axis=-1, keepdims=True)
    return inverse * (grad_norm - mean_grad - normed * mean_proj)


def f32(x):
    return x.astype(jnp.float32)


def bf16(x):
    return x.astype(jnp.bfloat16)


def round_kernel(x_ref, *refs):
    refs[-1][...] = x_ref[...].astype(jnp.bfloat16)


def rounded(x, *deps):
    n, d = x.shape
    block = n // 4
    return pl.pallas_call(
        round_kernel,
        grid=(4,),
        in_specs=[pl.BlockSpec((block, d), lambda i: (i, 0))]
        + [pl.BlockSpec(memory_space=pl.ANY)] * len(deps),
        out_specs=pl.BlockSpec((block, d), lambda i: (i, 0)),
        out_shape=jax.ShapeDtypeStruct((n, d), jnp.bfloat16),
    )(x, *deps)


def pack_kernel(*refs):
    row = 0
    for ref in refs[:-1]:
        refs[-1][row : row + ref.shape[0], :] = ref[...]
        row += ref.shape[0]


def pack(parts, d):
    parts = [x.reshape(-1, d) for x in parts]
    rows = sum(x.shape[0] for x in parts)
    return pl.pallas_call(
        pack_kernel,
        in_specs=[pl.BlockSpec(memory_space=pltpu.VMEM)] * len(parts),
        out_specs=pl.BlockSpec(memory_space=pltpu.VMEM),
        out_shape=jax.ShapeDtypeStruct((rows, d), jnp.float32),
    )(*parts)


def bias_kernel(scalars_ref, *refs, tp, heads, inward):
    z = scalars_ref[2]
    quads = PIECES // 2
    for t in range(tp):
        a = (z + tp - t) % tp
        shard = z ^ a if inward else a

        def move(x_ref, o_ref, there, here):
            if inward:
                there, here = here, there
            o_ref[pl.ds(there, 1), :] = x_ref[pl.ds(here, 1), :]

        for i in range(PIECES):
            for n in (0, 1):
                for h in range(heads):
                    there = (shard * heads + h) * PIECES + (i ^ scalars_ref[n])
                    move(refs[n], refs[n + 3], there, (t * heads + h) * PIECES + i)
                there = (shard * 2 + n) * PIECES + (i ^ scalars_ref[n])
                row = (((i // quads) * 2 + n) * quads + i % quads) * tp + t
                move(refs[2], refs[5], there, row)


def bias_rows(scalars, q, v, f, tp, heads, inward):
    return pl.pallas_call(
        partial(bias_kernel, tp=tp, heads=heads, inward=inward),
        in_specs=[pl.BlockSpec(memory_space=pltpu.SMEM)]
        + [pl.BlockSpec(memory_space=pltpu.VMEM)] * 3,
        out_specs=[pl.BlockSpec(memory_space=pltpu.VMEM)] * 3,
        out_shape=[jax.ShapeDtypeStruct(x.shape, x.dtype) for x in (q, v, f)],
    )(scalars, q, v, f)


def join_ffn_kernel(masks_ref, own_ref, mine_ref, other_ref, o_ref):
    mask = masks_ref[pl.program_id(0)]
    quads = mine_ref.shape[1]
    for i in range(2 * quads):
        o_ref[i // quads, 0, i % quads, 0] = own_ref[0, i ^ mask]
    o_ref[0, 0, :, 1:] = mine_ref[0, :, :, 0].astype(jnp.bfloat16)
    o_ref[1, 0, :, 1:] = other_ref[0, :, :, 0].astype(jnp.bfloat16)


def join_ffn(masks, own, mine, other, which):
    _, quads, others, _, n, d = mine.shape
    spec = pl.BlockSpec((1, quads, others, 1, n, d), lambda s, m: (s, 0, 0, which, 0, 0))
    return pl.pallas_call(
        join_ffn_kernel,
        grid_spec=pltpu.PrefetchScalarGridSpec(
            num_scalar_prefetch=1,
            grid=(2,),
            in_specs=[
                pl.BlockSpec((1, 2 * quads, n, d), lambda s, m: (s, 0, 0, 0)),
                spec,
                spec,
            ],
            out_specs=pl.BlockSpec(
                (2, 1, quads, others + 1, n, d), lambda s, m: (0, s, 0, 0, 0, 0)
            ),
        ),
        out_shape=jax.ShapeDtypeStruct((2, 2, quads, others + 1, n, d), jnp.bfloat16),
    )(masks, own, mine, other)


def join_att_kernel(masks_ref, own_ref, mine_ref, other_ref, o_ref):
    mask = masks_ref[pl.program_id(0)]
    _, _, heads, pieces, _, _ = own_ref.shape
    quads, others = mine_ref.shape[1:3]
    for h in range(heads):
        parts = [own_ref[0, 0, h, j ^ mask] for j in range(pieces)]
        o_ref[0, 0, 0, h] = jnp.concatenate(parts).astype(jnp.bfloat16)
        for t in range(others):
            parts = [ref[0, j, t, 0, h] for ref in (mine_ref, other_ref) for j in range(quads)]
            o_ref[0, 0, t + 1, h] = jnp.concatenate(parts).astype(jnp.bfloat16)


def join_att(masks, own, mine, other):
    _, quads, others, _, heads, e, d = mine.shape
    pieces = own.shape[3]
    spec = pl.BlockSpec((1, quads, others, 1, heads, e, d), lambda s, i, m: (s, 0, 0, i, 0, 0, 0))
    return pl.pallas_call(
        join_att_kernel,
        grid_spec=pltpu.PrefetchScalarGridSpec(
            num_scalar_prefetch=1,
            grid=(2, 2),
            in_specs=[
                pl.BlockSpec((1, 1, heads, pieces, e, d), lambda s, i, m: (s, i, 0, 0, 0, 0)),
                spec,
                spec,
            ],
            out_specs=pl.BlockSpec(
                (1, 1, others + 1, heads, pieces * e, d), lambda s, i, m: (s, i, 0, 0, 0, 0)
            ),
        ),
        out_shape=jax.ShapeDtypeStruct((2, 2, others + 1, heads, pieces * e, d), jnp.bfloat16),
    )(masks, own, mine, other)


def place_kernel(masks_ref, mine_ref, other_ref, o_ref):
    mask = masks_ref[pl.program_id(0)]
    quads = mine_ref.shape[1]
    for i in range(2 * quads):
        j = i ^ mask
        low = mine_ref[0, j & (quads - 1)]
        high = other_ref[0, j & (quads - 1)]
        o_ref[0, i] = jnp.where(j < quads, low, high)


def place(masks, mine, other):
    _, quads, n, d = mine.shape
    spec = pl.BlockSpec((1, quads, n, d), lambda s, m: (s, 0, 0, 0))
    return pl.pallas_call(
        place_kernel,
        grid_spec=pltpu.PrefetchScalarGridSpec(
            num_scalar_prefetch=1,
            grid=(2,),
            in_specs=[spec, spec],
            out_specs=pl.BlockSpec((1, 2 * quads, n, d), lambda s, m: (s, 0, 0, 0)),
        ),
        out_shape=jax.ShapeDtypeStruct((2, 2 * quads, n, d), jnp.float32),
    )(masks, mine, other)


def dot_t(a, b):
    return lax.dot_general(a, b, (((1,), (1,)), ((), ())), preferred_element_type=jnp.float32)


def dot_n(a, b):
    return lax.dot_general(a, b, (((1,), (0,)), ((), ())), preferred_element_type=jnp.float32)


def dot_a(a, b):
    return lax.dot_general(a, b, (((0,), (0,)), ((), ())), preferred_element_type=jnp.float32)


def make(mesh):
    rows = mesh.shape["rows"]
    T = mesh.shape["tp"]
    row_bits = rows.bit_length() - 1
    tp_bits = [1 << b for b in range(T.bit_length() - 1)]

    def swap(x, bit):
        return lax.ppermute(x, "rows", [(i, i ^ (1 << bit)) for i in range(rows)])

    def shift(x, k):
        return lax.ppermute(x, "tp", [(i, (i + k) % T) for i in range(T)])

    def shards(piece):
        others = [shift(piece, k) for k in range(1, T)]
        return [jnp.stack([x[s] for x in others]) for s in (0, 1)]

    def swap_first(bufs):
        return [jnp.stack([b, swap(b, bit)]) for b, bit in zip(bufs, (1, 2))]

    def swap_second(bufs):
        return jnp.stack([jnp.stack([b, swap(b, bit)]) for b, bit in zip(bufs, (2, 1))])

    def total_over(x):
        for bit in range(row_bits):
            x = x + swap(x, bit)
        for m in tp_bits:
            x = x + lax.ppermute(x, "tp", [(i, i ^ m) for i in range(T)])
        return x

    def halve_core(keep, send):
        return keep + swap(send, 0)

    def halve_first(both):
        return [both[s][0] + swap(both[s][1], bit) for s, bit in ((0, 2), (1, 1))]

    def halve_second(accs):
        return [acc[0] + swap(acc[1], bit) for acc, bit in zip(accs, (1, 2))]

    def shard_sum(accs):
        acc = jnp.stack(accs, axis=1)
        total = acc[0] + sum(shift(acc[T - k], k) for k in range(1, T))
        for bit in range(BITS, row_bits):
            total = total + swap(total, bit)
        return total

    def spread(total):
        both = swap_second(swap_first([total[0], total[1]]))
        both = both.reshape(2, PIECES // 2, total.shape[1], total.shape[2])
        return both, swap(both, 0)

    def per_device(
        features, type_ids, segment_ids, type_table, w_qkv, b_qv, w_out, b_out, gain_attn,
        shift_attn, w_up, b_up, w_down, b_down, gain_ffn, shift_ffn, cotangent,
    ):
        z = lax.axis_index("tp")
        r = lax.axis_index("rows")
        bits = [(r >> b) & 1 for b in range(BITS)]
        mask_a = bits[0] * 4 + bits[2] * 2 + bits[1]
        mask_b = bits[0] * 4 + bits[1] * 2 + bits[2]
        masks = (mask_a, mask_b)
        D = features.shape[1]
        width = w_qkv.shape[2]
        heads = width // HEAD_DIM
        shard_ff = w_up.shape[1]
        tokens = features.shape[0] // T
        length = segment_ids.shape[1]
        nrows = segment_ids.shape[0] // T
        E = HEAD_DIM // PIECES
        FP = shard_ff // (2 * PIECES)

        def own_slice(x, n):
            return lax.dynamic_slice_in_dim(x, z * n, n, 0)

        def pick(x, mask, axis):
            return lax.dynamic_index_in_dim(x, mask, axis, keepdims=False)

        quads = PIECES // 2
        scalars = jnp.stack([mask_a, mask_b, z]).astype(jnp.int32)
        masks_v = scalars
        na = 2 * heads * E
        att = jnp.concatenate([f32(jnp.swapaxes(w_qkv, 1, 2)), f32(w_out)[None]])
        att = att.reshape(2, 2, heads, PIECES, E, D)
        att_piece = jnp.stack([pick(att[s], masks[s], 2).reshape(na, D) for s in (0, 1)])
        att_bufs = shards(att_piece)
        small = jnp.concatenate([f32(b_qv).reshape(-1), f32(b_up)])[None]
        for m in tp_bits:
            small = jnp.concatenate(
                [small, lax.ppermute(small, "tp", [(i, i ^ m) for i in range(T)])]
            )
        up_own = w_up.T.reshape(2, PIECES, FP, D)
        down_own = w_down.reshape(2, PIECES, FP, D)
        ffn_piece = jnp.stack(
            [
                jnp.concatenate([f32(pick(up_own[s], masks[s], 0)), f32(pick(down_own[s], masks[s], 0))])
                for s in (0, 1)
            ]
        )
        ffn_piece, *att_bufs = lax.optimization_barrier((ffn_piece, *att_bufs))
        ffn_bufs = shards(ffn_piece)
        shape = (2, quads, T - 1, 2, heads, E, D)
        both = swap_second(swap_first(att_bufs))
        other = swap(both, 0).reshape(shape)
        att_w = join_att(masks_v, att, both.reshape(shape), other)
        att_w = att_w.reshape(4 * T * width, D)
        wqkv_t = att_w[: 3 * T * width]
        wo = att_w[3 * T * width :]

        bq, bv, bup = bias_rows(
            scalars,
            small[:, :width].reshape(-1, E),
            small[:, width : 2 * width].reshape(-1, E),
            small[:, 2 * width :].reshape(-1, FP),
            T, heads, True,
        )
        bq, bv, bup = bq.reshape(-1), bv.reshape(-1), bup.reshape(-1)

        type_frac = f32(own_slice(type_ids, tokens))[:, None]
        segment = own_slice(segment_ids, nrows)
        table = f32(type_table)
        embedded = f32(own_slice(features, tokens)) + (table[0] + type_frac * (table[1] - table[0]))
        normal_in = bf16(embedded)
        C = T * width
        H = T * heads
        shape_four = (nrows, length, H, HEAD_DIM)
        ffn_both = swap_second(swap_first(ffn_bufs))
        queries = bf16(dot_t(normal_in, wqkv_t[:C]) + bq).reshape(shape_four)
        keys = bf16(dot_t(normal_in, wqkv_t[C : 2 * C])).reshape(shape_four)
        values = bf16(dot_t(normal_in, wqkv_t[2 * C :]) + bv).reshape(shape_four)
        scale = HEAD_DIM ** (-0.5)
        same = (segment[:, :, None] == segment[:, None, :])[:, None]
        scores = jnp.einsum("rqhd,rkhd->rhqk", queries, keys, preferred_element_type=jnp.float32)
        scores = jnp.where(same, scores * scale, NEG)
        highest = jnp.max(scores, axis=-1, keepdims=True)
        weights = jnp.exp(scores - highest)
        total = jnp.sum(weights, axis=-1, keepdims=True)
        weights = bf16(weights / total)
        attended = bf16(
            jnp.einsum("rhqk,rkhd->rqhd", weights, values, preferred_element_type=jnp.float32)
        ).reshape(tokens, C)
        ffn_other = swap(ffn_both, 0)
        shape = (2, quads, T - 1, 2, FP, D)
        up_t, down = (
            join_ffn(masks_v, own, ffn_both.reshape(shape), ffn_other.reshape(shape), i).reshape(-1, D)
            for i, own in enumerate((up_own, down_own))
        )
        attn_out = dot_n(attended, wo) + f32(b_out)
        normed_a, inverse_a = normalize(embedded + attn_out)
        gain_one = f32(gain_attn)
        normed_one = normed_a * gain_one + f32(shift_attn)
        ffn_in = bf16(normed_one)
        pre_act = dot_t(ffn_in, up_t) + bup
        cdf = 0.5 * (1.0 + lax.erf(pre_act * (0.5**0.5)))
        activated = bf16(pre_act * cdf)
        ffn_out = dot_n(activated, down) + f32(b_down)
        normed_b, inverse_b = normalize(normed_one + ffn_out)
        gain_two = f32(gain_ffn)
        out_own = normed_b * gain_two + f32(shift_ffn)
        gathered_out = lax.all_gather(out_own, "tp", axis=0, tiled=True)
        output = rounded(gathered_out)

        grad_out = f32(own_slice(cotangent, tokens))
        grad_shift_ffn = jnp.sum(grad_out, axis=0)
        grad_gain_ffn = jnp.sum(grad_out * normed_b, axis=0)
        grad_h2 = norm_back(grad_out * gain_two, normed_b, inverse_b)
        grad_b_down = jnp.sum(grad_h2, axis=0)
        grad_h2_low = bf16(grad_h2)
        half = T * shard_ff // 2
        six = (2, 2, 2, T, FP, D)
        gd_send = dot_a(activated[:, half:], grad_h2_low).reshape(six)
        gd_keep = dot_a(activated[:, :half], grad_h2_low).reshape(six)
        gd = halve_core(gd_keep, gd_send)
        gd = halve_second(halve_first(gd))
        grad_act = dot_t(grad_h2_low, down)
        pdf = jnp.exp(-0.5 * pre_act * pre_act) * (0.5 / jnp.pi) ** 0.5
        grad_pre = bf16(grad_act * (cdf + pre_act * pdf))
        grad_b_up = jnp.sum(f32(grad_pre), axis=0)
        gu_send = dot_a(grad_pre[:, half:], ffn_in).reshape(six)
        gu_keep = dot_a(grad_pre[:, :half], ffn_in).reshape(six)
        gu = halve_core(gu_keep, gu_send)
        gu = halve_second(halve_first(gu))
        gf = shard_sum([jnp.concatenate([u, d], axis=1) for u, d in zip(gu, gd)])
        grad_normed = grad_h2 + dot_n(grad_pre, up_t)
        grad_shift_attn = jnp.sum(grad_normed, axis=0)
        grad_gain_attn = jnp.sum(grad_normed * normed_a, axis=0)
        grad_h1 = norm_back(grad_normed * gain_one, normed_a, inverse_a)
        grad_b_out = jnp.sum(grad_h1, axis=0)
        grad_h1_low = bf16(grad_h1)
        grad_wo = dot_a(attended, grad_h1_low)
        grad_att = bf16(dot_t(grad_h1_low, wo)).reshape(shape_four)
        logsum = highest + jnp.log(total)
        probs = jnp.exp(scores - logsum)
        grad_weights = jnp.einsum(
            "rqhd,rkhd->rhqk", grad_att, values, preferred_element_type=jnp.float32
        )
        inner = jnp.sum(probs * grad_weights, axis=-1, keepdims=True)
        grad_scores = bf16(probs * (grad_weights - inner))
        grad_q = bf16(
            jnp.einsum("rhqk,rkhd->rqhd", grad_scores, keys, preferred_element_type=jnp.float32)
            * scale
        ).reshape(tokens, C)
        grad_k = bf16(
            jnp.einsum("rhqk,rqhd->rkhd", grad_scores, queries, preferred_element_type=jnp.float32)
            * scale
        ).reshape(tokens, C)
        grad_v = bf16(
            jnp.einsum("rhqk,rqhd->rkhd", bf16(probs), grad_att, preferred_element_type=jnp.float32)
        ).reshape(tokens, C)
        grad_proj = jnp.concatenate([grad_q, grad_k, grad_v], axis=1)
        grad_embedded = lax.optimization_barrier(grad_h1 + dot_n(grad_proj, wqkv_t))
        gathered = lax.all_gather(grad_embedded, "tp", axis=0, tiled=True)
        gq = dot_a(grad_proj, normal_in)
        ga = jnp.concatenate([gq, grad_wo]).reshape(2, 2, T, heads, 2, 2, 2, E, D)
        ga = ga.transpose(4, 0, 5, 6, 2, 1, 3, 7, 8).reshape(2, 2, 2, 2, T, na, D)
        ga = halve_second(halve_first(halve_core(ga[0], ga[1])))
        ga = shard_sum(ga)

        pieces = spread(gf)
        g_ffn = place(masks_v, *pieces)
        grad_w_up = g_ffn[:, :, :FP].reshape(shard_ff, D).T
        grad_w_down = g_ffn[:, :, FP:].reshape(shard_ff, D)
        g_att = place(masks_v, *spread(ga)).reshape(2, PIECES, 2, heads, E, D)
        g_att = g_att.transpose(0, 2, 3, 1, 4, 5).reshape(4, width, D)
        grad_qkv = jnp.swapaxes(g_att[:3], 1, 2)
        grad_w_out = g_att[3]

        gbq, gbv, gbup = bias_rows(
            scalars,
            jnp.sum(f32(grad_q), axis=0).reshape(-1, E),
            jnp.sum(f32(grad_v), axis=0).reshape(-1, E),
            grad_b_up.reshape(-1, FP),
            T, heads, False,
        )
        upper = jnp.sum(type_frac * grad_embedded, axis=0)
        lower = jnp.sum(grad_embedded, axis=0) - upper
        vec = pack(
            [
                lower, upper, grad_b_out, grad_gain_attn, grad_shift_attn, grad_b_down,
                grad_gain_ffn, grad_shift_ffn, gbq.reshape(-1), gbv.reshape(-1), gbup.reshape(-1),
            ],
            D,
        )
        vec = total_over(vec).reshape(-1)
        grad_features = rounded(gathered, vec, output, g_ffn)
        lines = vec[: 8 * D].reshape(8, D)
        gb = vec[8 * D : 8 * D + 2 * C].reshape(2, C)
        grad_bias_qv = lax.dynamic_slice_in_dim(gb, z * width, width, 1)
        grad_b_up = lax.dynamic_slice_in_dim(vec[8 * D + 2 * C :], z * shard_ff, shard_ff, 0)
        return (
            output, grad_features, lines[:2], grad_qkv, grad_bias_qv, grad_w_out, lines[2],
            lines[3], lines[4], grad_w_up, grad_b_up, grad_w_down, lines[5], lines[6], lines[7],
        )

    return per_device


def solution(mesh):
    in_specs = (
        P("rows", None), P("rows"), P("rows", None), P(), P(None, None, "tp"), P(None, "tp"),
        P("tp", None), P(), P(), P(), P(None, "tp"), P("tp"), P("tp", None), P(), P(), P(),
        P("rows", None),
    )
    out_specs = (
        P("rows", None), P("rows", None), P(), P(None, None, "tp"), P(None, "tp"), P("tp", None),
        P(), P(), P(), P(None, "tp"), P("tp"), P("tp", None), P(), P(), P(),
    )
    layer = make(mesh)

    return jax.shard_map(layer, mesh=mesh, in_specs=in_specs, out_specs=out_specs, check_vma=False)
```

```python
from functools import partial

import jax
import jax.numpy as jnp
from jax import lax
from jax.experimental import pallas as pl
from jax.experimental.pallas import tpu as pltpu
from jax.sharding import PartitionSpec as P


HEAD_DIM = 64
BITS = 3
PIECES = 1 << BITS
NEG = -1000000000.0


def normalize(hidden):
    center = hidden - jnp.mean(hidden, axis=-1, keepdims=True)
    variance = jnp.mean(center * center, axis=-1, keepdims=True)
    inverse = lax.rsqrt(variance + 1e-05)
    return (center * inverse, inverse)


def norm_back(grad_norm, normed, inverse):
    mean_grad = jnp.mean(grad_norm, axis=-1, keepdims=True)
    mean_proj = jnp.mean(grad_norm * normed, axis=-1, keepdims=True)
    return inverse * (grad_norm - mean_grad - normed * mean_proj)


def f32(x):
    return x.astype(jnp.float32)


def bf16(x):
    return x.astype(jnp.bfloat16)


def round_kernel(x_ref, *refs):
    refs[-1][...] = x_ref[...].astype(jnp.bfloat16)


def rounded(x, *deps):
    n, d = x.shape
    block = n // 4
    return pl.pallas_call(
        round_kernel,
        grid=(4,),
        in_specs=[pl.BlockSpec((block, d), lambda i: (i, 0))]
        + [pl.BlockSpec(memory_space=pl.ANY)] * len(deps),
        out_specs=pl.BlockSpec((block, d), lambda i: (i, 0)),
        out_shape=jax.ShapeDtypeStruct((n, d), jnp.bfloat16),
    )(x, *deps)


def sum_kernel(a_ref, ra_ref, b_ref, rb_ref, o_ref):
    o_ref[:, 0] = a_ref[0] + ra_ref[...]
    o_ref[:, 1] = b_ref[0] + rb_ref[...]


def sum_sets(accs, received):
    _, t, n, d = accs[0].shape
    kept = pl.BlockSpec((1, t, n, d), lambda i: (0, 0, 0, 0))
    other = pl.BlockSpec((t, n, d), lambda i: (0, 0, 0))
    return pl.pallas_call(
        sum_kernel,
        grid=(1,),
        in_specs=[kept, other, kept, other],
        out_specs=pl.BlockSpec((t, 2, n, d), lambda i: (0, 0, 0, 0)),
        out_shape=jax.ShapeDtypeStruct((t, 2, n, d), jnp.float32),
    )(accs[0], received[0], accs[1], received[1])


def pack_kernel(*refs):
    row = 0
    for ref in refs[:-1]:
        refs[-1][row : row + ref.shape[0], :] = ref[...]
        row += ref.shape[0]


def pack(parts, d):
    parts = [x.reshape(-1, d) for x in parts]
    rows = sum(x.shape[0] for x in parts)
    return pl.pallas_call(
        pack_kernel,
        in_specs=[pl.BlockSpec(memory_space=pltpu.VMEM)] * len(parts),
        out_specs=pl.BlockSpec(memory_space=pltpu.VMEM),
        out_shape=jax.ShapeDtypeStruct((rows, d), jnp.float32),
    )(*parts)


def bias_kernel(scalars_ref, *refs, tp, heads, inward):
    z = scalars_ref[2]
    quads = PIECES // 2
    for t in range(tp):
        a = (z + tp - t) % tp
        shard = z ^ a if inward else a

        def move(x_ref, o_ref, there, here):
            if inward:
                there, here = here, there
            o_ref[pl.ds(there, 1), :] = x_ref[pl.ds(here, 1), :]

        for i in range(PIECES):
            for n in (0, 1):
                for h in range(heads):
                    there = (shard * heads + h) * PIECES + (i ^ scalars_ref[n])
                    move(refs[n], refs[n + 3], there, (t * heads + h) * PIECES + i)
                there = (shard * 2 + n) * PIECES + (i ^ scalars_ref[n])
                row = (((i // quads) * 2 + n) * quads + i % quads) * tp + t
                move(refs[2], refs[5], there, row)


def bias_rows(scalars, q, v, f, tp, heads, inward):
    return pl.pallas_call(
        partial(bias_kernel, tp=tp, heads=heads, inward=inward),
        in_specs=[pl.BlockSpec(memory_space=pltpu.SMEM)]
        + [pl.BlockSpec(memory_space=pltpu.VMEM)] * 3,
        out_specs=[pl.BlockSpec(memory_space=pltpu.VMEM)] * 3,
        out_shape=[jax.ShapeDtypeStruct(x.shape, x.dtype) for x in (q, v, f)],
    )(scalars, q, v, f)


def join_ffn_kernel(masks_ref, own_ref, mine_ref, other_ref, o_ref):
    mask = masks_ref[pl.program_id(0)]
    quads = mine_ref.shape[1]
    for i in range(2 * quads):
        o_ref[i // quads, 0, i % quads, 0] = own_ref[0, i ^ mask]
    o_ref[0, 0, :, 1:] = mine_ref[0, :, :, 0].astype(jnp.bfloat16)
    o_ref[1, 0, :, 1:] = other_ref[0, :, :, 0].astype(jnp.bfloat16)


def join_ffn(masks, own, mine, other):
    _, quads, others, _, n, d = mine.shape
    spec = pl.BlockSpec((1, quads, others, 1, n, d), lambda s, m: (s, 0, 0, 0, 0, 0))
    return pl.pallas_call(
        join_ffn_kernel,
        grid_spec=pltpu.PrefetchScalarGridSpec(
            num_scalar_prefetch=1,
            grid=(2,),
            in_specs=[
                pl.BlockSpec((1, 2 * quads, n, d), lambda s, m: (s, 0, 0, 0)),
                spec,
                spec,
            ],
            out_specs=pl.BlockSpec(
                (2, 1, quads, others + 1, n, d), lambda s, m: (0, s, 0, 0, 0, 0)
            ),
        ),
        out_shape=jax.ShapeDtypeStruct((2, 2, quads, others + 1, n, d), jnp.bfloat16),
    )(masks, own, mine, other)


def join_att_kernel(masks_ref, own_ref, mine_ref, other_ref, o_ref):
    mask = masks_ref[pl.program_id(0)]
    _, _, heads, pieces, _, _ = own_ref.shape
    quads, others = mine_ref.shape[1:3]
    for h in range(heads):
        parts = [own_ref[0, 0, h, j ^ mask] for j in range(pieces)]
        o_ref[0, 0, 0, h] = jnp.concatenate(parts).astype(jnp.bfloat16)
        for t in range(others):
            parts = [ref[0, j, t, 0, h] for ref in (mine_ref, other_ref) for j in range(quads)]
            o_ref[0, 0, t + 1, h] = jnp.concatenate(parts).astype(jnp.bfloat16)


def join_att(masks, own, mine, other):
    _, quads, others, _, heads, e, d = mine.shape
    pieces = own.shape[3]
    spec = pl.BlockSpec((1, quads, others, 1, heads, e, d), lambda s, i, m: (s, 0, 0, i, 0, 0, 0))
    return pl.pallas_call(
        join_att_kernel,
        grid_spec=pltpu.PrefetchScalarGridSpec(
            num_scalar_prefetch=1,
            grid=(2, 2),
            in_specs=[
                pl.BlockSpec((1, 1, heads, pieces, e, d), lambda s, i, m: (s, i, 0, 0, 0, 0)),
                spec,
                spec,
            ],
            out_specs=pl.BlockSpec(
                (1, 1, others + 1, heads, pieces * e, d), lambda s, i, m: (s, i, 0, 0, 0, 0)
            ),
        ),
        out_shape=jax.ShapeDtypeStruct((2, 2, others + 1, heads, pieces * e, d), jnp.bfloat16),
    )(masks, own, mine, other)


def place_kernel(masks_ref, mine_ref, other_ref, o_ref):
    mask = masks_ref[pl.program_id(0)]
    quads = mine_ref.shape[1]
    for i in range(2 * quads):
        j = i ^ mask
        low = mine_ref[0, j & (quads - 1)]
        high = other_ref[0, j & (quads - 1)]
        o_ref[0, i] = jnp.where(j < quads, low, high)


def place(masks, mine, other):
    _, quads, n, d = mine.shape
    spec = pl.BlockSpec((1, quads, n, d), lambda s, m: (s, 0, 0, 0))
    return pl.pallas_call(
        place_kernel,
        grid_spec=pltpu.PrefetchScalarGridSpec(
            num_scalar_prefetch=1,
            grid=(2,),
            in_specs=[spec, spec],
            out_specs=pl.BlockSpec((1, 2 * quads, n, d), lambda s, m: (s, 0, 0, 0)),
        ),
        out_shape=jax.ShapeDtypeStruct((2, 2 * quads, n, d), jnp.float32),
    )(masks, mine, other)


def dot_t(a, b):
    return lax.dot_general(a, b, (((1,), (1,)), ((), ())), preferred_element_type=jnp.float32)


def dot_n(a, b):
    return lax.dot_general(a, b, (((1,), (0,)), ((), ())), preferred_element_type=jnp.float32)


def dot_a(a, b):
    return lax.dot_general(a, b, (((0,), (0,)), ((), ())), preferred_element_type=jnp.float32)


def make(mesh):
    rows = mesh.shape["rows"]
    T = mesh.shape["tp"]
    row_bits = rows.bit_length() - 1
    tp_bits = [1 << b for b in range(T.bit_length() - 1)]

    def swap(x, bit):
        return lax.ppermute(x, "rows", [(i, i ^ (1 << bit)) for i in range(rows)])

    def shift(x, k):
        return lax.ppermute(x, "tp", [(i, (i + k) % T) for i in range(T)])

    def shards(piece):
        others = [shift(piece, k) for k in range(1, T)]
        return [jnp.stack([x[s] for x in others]) for s in (0, 1)]

    def swap_first(bufs):
        return [jnp.stack([b, swap(b, bit)]) for b, bit in zip(bufs, (1, 2))]

    def swap_second(bufs):
        return jnp.stack([jnp.stack([b, swap(b, bit)]) for b, bit in zip(bufs, (2, 1))])

    def total_over(x):
        x = x + sum(shift(x, k) for k in range(1, T))
        for bit in range(row_bits):
            x = x + swap(x, bit)
        return x

    def halve_core(keep, send):
        return keep + swap(send, 0)

    def halve_first(both):
        return [both[s][0] + swap(both[s][1], bit) for s, bit in ((0, 2), (1, 1))]

    def halve_second(accs):
        return [acc[0] + swap(acc[1], bit) for acc, bit in zip(accs, (1, 2))]

    def shard_sum(acc):
        total = acc[0] + sum(shift(acc[T - k], k) for k in range(1, T))
        return more(total)

    def more(total):
        for bit in range(BITS, row_bits):
            total = total + swap(total, bit)
        return total

    def spread(total):
        both = swap_second(swap_first([total[0], total[1]]))
        both = both.reshape(2, PIECES // 2, total.shape[1], total.shape[2])
        return both, swap(both, 0)

    def per_device(
        features, type_ids, segment_ids, type_table, w_qkv, b_qv, w_out, b_out, gain_attn,
        shift_attn, w_up, b_up, w_down, b_down, gain_ffn, shift_ffn, cotangent,
    ):
        z = lax.axis_index("tp")
        r = lax.axis_index("rows")
        bits = [(r >> b) & 1 for b in range(BITS)]
        mask_a = bits[0] * 4 + bits[2] * 2 + bits[1]
        mask_b = bits[0] * 4 + bits[1] * 2 + bits[2]
        masks = (mask_a, mask_b)
        D = features.shape[1]
        width = w_qkv.shape[2]
        heads = width // HEAD_DIM
        shard_ff = w_up.shape[1]
        tokens = features.shape[0] // T
        length = segment_ids.shape[1]
        nrows = segment_ids.shape[0] // T
        E = HEAD_DIM // PIECES
        FP = shard_ff // (2 * PIECES)

        def own_slice(x, n):
            return lax.dynamic_slice_in_dim(x, z * n, n, 0)

        def pick(x, mask, axis):
            return lax.dynamic_index_in_dim(x, mask, axis, keepdims=False)

        quads = PIECES // 2
        scalars = jnp.stack([mask_a, mask_b, z]).astype(jnp.int32)
        masks_v = scalars
        na = 2 * heads * E
        att = jnp.concatenate([f32(jnp.swapaxes(w_qkv, 1, 2)), f32(w_out)[None]])
        att = att.reshape(2, 2, heads, PIECES, E, D)
        att_piece = jnp.stack([pick(att[s], masks[s], 2).reshape(na, D) for s in (0, 1)])
        att_bufs = shards(att_piece)
        small = jnp.concatenate([f32(b_qv).reshape(-1), f32(b_up)])[None]
        for m in tp_bits:
            other = lax.ppermute(small, "tp", [(i, i ^ m) for i in range(T)])
            small = jnp.concatenate([small, other])
        up_own = w_up.T.reshape(2, PIECES, FP, D)
        down_own = w_down.reshape(2, PIECES, FP, D)
        up_piece, down_piece = (
            jnp.stack([f32(pick(own[s], masks[s], 0)) for s in (0, 1)])
            for own in (up_own, down_own)
        )
        up_piece, down_piece, *att_bufs = lax.optimization_barrier(
            (up_piece, down_piece, *att_bufs)
        )
        up_bufs, down_bufs = shards(up_piece), shards(down_piece)
        shape = (2, quads, T - 1, 2, heads, E, D)
        both = swap_second(swap_first(att_bufs))
        other = swap(both, 0).reshape(shape)
        att_w = join_att(masks_v, att, both.reshape(shape), other)
        att_w = att_w.reshape(4 * T * width, D)
        wqkv_t = att_w[: 3 * T * width]
        wo = att_w[3 * T * width :]

        bq, bv, bup = bias_rows(
            scalars,
            small[:, :width].reshape(-1, E),
            small[:, width : 2 * width].reshape(-1, E),
            small[:, 2 * width :].reshape(-1, FP),
            T, heads, True,
        )
        bq, bv, bup = bq.reshape(-1), bv.reshape(-1), bup.reshape(-1)

        out_bias, down_bias = f32(b_out), f32(b_down)
        gain_one, gain_two = f32(gain_attn), f32(gain_ffn)
        shift_one, shift_two = f32(shift_attn), f32(shift_ffn)
        type_frac = f32(own_slice(type_ids, tokens))[:, None]
        segment = own_slice(segment_ids, nrows)
        table = f32(type_table)
        embedded = f32(own_slice(features, tokens))
        embedded = embedded + (table[0] + type_frac * (table[1] - table[0]))
        normal_in = bf16(embedded)
        C = T * width
        H = T * heads
        shape_four = (nrows, length, H, HEAD_DIM)
        up_both = swap_second(swap_first(up_bufs))
        down_both = swap_second(swap_first(down_bufs))
        queries = bf16(dot_t(normal_in, wqkv_t[:C]) + bq).reshape(shape_four)
        keys = bf16(dot_t(normal_in, wqkv_t[C : 2 * C])).reshape(shape_four)
        values = bf16(dot_t(normal_in, wqkv_t[2 * C :]) + bv).reshape(shape_four)
        scale = HEAD_DIM ** (-0.5)
        same = (segment[:, :, None] == segment[:, None, :])[:, None]
        scores = jnp.einsum("rqhd,rkhd->rhqk", queries, keys, preferred_element_type=jnp.float32)
        scores = jnp.where(same, scores * scale, NEG)
        highest = jnp.max(scores, axis=-1, keepdims=True)
        weights = jnp.exp(scores - highest)
        total = jnp.sum(weights, axis=-1, keepdims=True)
        weights = bf16(weights / total)
        attended = bf16(
            jnp.einsum("rhqk,rkhd->rqhd", weights, values, preferred_element_type=jnp.float32)
        ).reshape(tokens, C)
        shape = (2, quads, T - 1, 1, FP, D)
        up_t, down = (
            join_ffn(masks_v, own, both.reshape(shape), swap(both, 0).reshape(shape)).reshape(-1, D)
            for own, both in ((up_own, up_both), (down_own, down_both))
        )
        attn_out = dot_n(attended, wo) + out_bias
        normed_a, inverse_a = normalize(embedded + attn_out)
        normed_one = normed_a * gain_one + shift_one
        ffn_in = bf16(normed_one)
        pre_act = dot_t(ffn_in, up_t) + bup
        cdf = 0.5 * (1.0 + lax.erf(pre_act * (0.5**0.5)))
        activated = bf16(pre_act * cdf)
        ffn_out = dot_n(activated, down) + down_bias
        normed_b, inverse_b = normalize(normed_one + ffn_out)
        out_own = normed_b * gain_two + shift_two
        gathered_out = lax.all_gather(out_own, "tp", axis=0, tiled=True)
        output = rounded(gathered_out)

        grad_out = f32(own_slice(cotangent, tokens))
        grad_shift_ffn = jnp.sum(grad_out, axis=0)
        grad_gain_ffn = jnp.sum(grad_out * normed_b, axis=0)
        grad_h2 = norm_back(grad_out * gain_two, normed_b, inverse_b)
        grad_b_down = jnp.sum(grad_h2, axis=0)
        grad_h2_low = bf16(grad_h2)
        half = T * shard_ff // 2
        six = (2, 2, 2, T, FP, D)
        gd_send = dot_a(activated[:, half:], grad_h2_low).reshape(six)
        gd_keep = dot_a(activated[:, :half], grad_h2_low).reshape(six)
        gd = halve_core(gd_keep, gd_send)
        gd = halve_second(halve_first(gd))
        grad_act = dot_t(grad_h2_low, down)
        pdf = jnp.exp(-0.5 * pre_act * pre_act) * (0.5 / jnp.pi) ** 0.5
        grad_pre = bf16(grad_act * (cdf + pre_act * pdf))
        grad_b_up = jnp.sum(f32(grad_pre), axis=0)
        gu_send = dot_a(grad_pre[:, half:], ffn_in).reshape(six)
        gu_keep = dot_a(grad_pre[:, :half], ffn_in).reshape(six)
        gu = halve_core(gu_keep, gu_send)
        gu = halve_second(halve_first(gu))
        gf = shard_sum(jnp.stack([jnp.concatenate([u, d], axis=1) for u, d in zip(gu, gd)], axis=1))
        grad_normed = grad_h2 + dot_n(grad_pre, up_t)
        grad_shift_attn = jnp.sum(grad_normed, axis=0)
        grad_gain_attn = jnp.sum(grad_normed * normed_a, axis=0)
        grad_h1 = norm_back(grad_normed * gain_one, normed_a, inverse_a)
        grad_b_out = jnp.sum(grad_h1, axis=0)
        grad_h1_low = bf16(grad_h1)
        grad_wo = dot_a(attended, grad_h1_low)
        grad_att = bf16(dot_t(grad_h1_low, wo)).reshape(shape_four)
        logsum = highest + jnp.log(total)
        probs = jnp.exp(scores - logsum)
        grad_weights = jnp.einsum(
            "rqhd,rkhd->rhqk", grad_att, values, preferred_element_type=jnp.float32
        )
        inner = jnp.sum(probs * grad_weights, axis=-1, keepdims=True)
        grad_scores = bf16(probs * (grad_weights - inner))
        grad_q = bf16(
            jnp.einsum("rhqk,rkhd->rqhd", grad_scores, keys, preferred_element_type=jnp.float32)
            * scale
        ).reshape(tokens, C)
        grad_k = bf16(
            jnp.einsum("rhqk,rqhd->rkhd", grad_scores, queries, preferred_element_type=jnp.float32)
            * scale
        ).reshape(tokens, C)
        grad_v = bf16(
            jnp.einsum("rhqk,rqhd->rkhd", bf16(probs), grad_att, preferred_element_type=jnp.float32)
        ).reshape(tokens, C)
        grad_proj = jnp.concatenate([grad_q, grad_k, grad_v], axis=1)
        grad_embedded = lax.optimization_barrier(grad_h1 + dot_n(grad_proj, wqkv_t))
        gathered = lax.all_gather(grad_embedded, "tp", axis=0, tiled=True)
        gq = dot_a(grad_proj, normal_in)
        ga = jnp.concatenate([gq, grad_wo]).reshape(2, 2, T, heads, 2, 2, 2, E, D)
        ga = ga.transpose(4, 0, 5, 6, 2, 1, 3, 7, 8).reshape(2, 2, 2, 2, T, na, D)
        ga = halve_first(halve_core(ga[0], ga[1]))
        received = [swap(acc[1], bit) for acc, bit in zip(ga, (1, 2))]
        ga = sum_sets(ga, received)
        ga = shard_sum(ga)

        pieces = spread(gf)
        g_ffn = place(masks_v, *pieces)
        grad_w_up = g_ffn[:, :, :FP].reshape(shard_ff, D).T
        grad_w_down = g_ffn[:, :, FP:].reshape(shard_ff, D)
        g_att = place(masks_v, *spread(ga)).reshape(2, PIECES, 2, heads, E, D)
        g_att = g_att.transpose(0, 2, 3, 1, 4, 5).reshape(4, width, D)
        grad_qkv = jnp.swapaxes(g_att[:3], 1, 2)
        grad_w_out = g_att[3]

        gbq, gbv, gbup = bias_rows(
            scalars,
            jnp.sum(f32(grad_q), axis=0).reshape(-1, E),
            jnp.sum(f32(grad_v), axis=0).reshape(-1, E),
            grad_b_up.reshape(-1, FP),
            T, heads, False,
        )
        upper = jnp.sum(type_frac * grad_embedded, axis=0)
        lower = jnp.sum(grad_embedded, axis=0) - upper
        vec = pack(
            [
                lower, upper, grad_b_out, grad_gain_attn, grad_shift_attn, grad_b_down,
                grad_gain_ffn, grad_shift_ffn, gbq.reshape(-1), gbv.reshape(-1), gbup.reshape(-1),
            ],
            D,
        )
        vec = total_over(vec).reshape(-1)
        grad_features = rounded(gathered, vec, output, g_ffn)
        lines = vec[: 8 * D].reshape(8, D)
        gb = vec[8 * D : 8 * D + 2 * C].reshape(2, C)
        grad_bias_qv = lax.dynamic_slice_in_dim(gb, z * width, width, 1)
        grad_b_up = lax.dynamic_slice_in_dim(vec[8 * D + 2 * C :], z * shard_ff, shard_ff, 0)
        return (
            output, grad_features, lines[:2], grad_qkv, grad_bias_qv, grad_w_out, lines[2],
            lines[3], lines[4], grad_w_up, grad_b_up, grad_w_down, lines[5], lines[6], lines[7],
        )

    return per_device


def solution(mesh):
    in_specs = (
        P("rows", None), P("rows"), P("rows", None), P(), P(None, None, "tp"), P(None, "tp"),
        P("tp", None), P(), P(), P(), P(None, "tp"), P("tp"), P("tp", None), P(), P(), P(),
        P("rows", None),
    )
    out_specs = (
        P("rows", None), P("rows", None), P(), P(None, None, "tp"), P(None, "tp"), P("tp", None),
        P(), P(), P(), P(None, "tp"), P("tp"), P("tp", None), P(), P(), P(),
    )
    layer = make(mesh)

    return jax.shard_map(layer, mesh=mesh, in_specs=in_specs, out_specs=out_specs, check_vma=False)
```
